32 devices in a mesh: dp: 2 (over core), node: 4 (over y, x), pipe: 4 (over z).
Axes of the slice: x: 2, y: 2, z: 4, core: 2. Of those that a mesh axis runs over, the one named last changes fastest.
Arguments:
- final_hidden: bfloat16 [4096, 8192], P(('dp', 'node', 'pipe')), may hold values from -128 to 128
- value_head: bfloat16 [8192, 128], replicated, may hold values from -3 to 3
- norm_gain: bfloat16 [8192], replicated, may hold values from 0.5 to 1.5
- rewards: float32 [4096], P(('dp', 'node', 'pipe')), may hold values from -6 to 6
- old_values: float32 [4096], P(('dp', 'node', 'pipe')), may hold values from -6 to 6
- loss_mask: int32 [4096], P(('dp', 'node', 'pipe')), may hold values 0 or 1
- row_exp: int32 [32, 8192], P(('dp', 'node', 'pipe')), may hold values from -14 to -11
- gain_exp: int32 [32, 64], P(('dp', 'node', 'pipe')), may hold values from -16 to -7
- first_w: float32 [8192, 128], P(('dp', 'node', 'pipe')), may hold values from -4 to 4
- second_w: float32 [8192, 128], P(('dp', 'node', 'pipe')), may hold values from 0.01 to 1
- first_g: float32 [8192], P(('dp', 'node', 'pipe')), may hold values from -4 to 4
- second_g: float32 [8192], P(('dp', 'node', 'pipe')), may hold values from 0.01 to 1
Outputs:
- new_weight: bfloat16 [8192, 128], P(('dp', 'node'))
- new_gain: bfloat16 [8192], P(('dp', 'node'))
- first_w_new: float32 [8192, 128], P(('dp', 'node', 'pipe'))
- second_w_new: float32 [8192, 128], P(('dp', 'node', 'pipe'))
- first_g_new: float32 [8192], P(('dp', 'node', 'pipe'))
- second_g_new: float32 [8192], P(('dp', 'node', 'pipe'))
The draws below stay inside these ranges and needn't reach their ends.
All inputs are finite; a program needn't handle non-finite values. No bound on the sum of `loss_mask` on one device may be relied on, other than what follows from the above.
Results may differ from the reference program's by a relative error of at most 0.0055.
Values may be sent and summed in bfloat16 or wider, within the bound.
A program may use at most 64 MiB of HBM per device.

```python
import math
import jax
import jax.numpy as jnp
from jax import lax

D = 8192
BINS = 128
GBLK = 128
SEQ = 32
T_DEV = 128
GROUPS = 32
TOKENS = 4096
N_DP = 2
N_NODE = 4
N_PIPE = 4


def head_columns(key):
    return 0.4 * jax.random.truncated_normal(jax.random.fold_in(key, 101), -6.0, 6.0, (D, BINS), jnp.float32)


def draw_value_head(key, part):
    return head_columns(key).astype(jnp.bfloat16)


def draw_final_hidden(key, part):
    drawn = jax.random.truncated_normal(jax.random.fold_in(key, 202), -6.0, 6.0, (TOKENS, D), jnp.float32)
    return drawn.astype(jnp.bfloat16)


def touch_ends(values, key, low, high):
    extent = values.shape
    spot = [jax.random.randint(jax.random.fold_in(key, axis), (), 0, extent[axis]) for axis in range(len(extent))]
    values = values.at[tuple(spot)].set(low)
    longest = extent.index(max(extent))
    spot[longest] = (spot[longest] + 1) % extent[longest]
    return values.at[tuple(spot)].set(high)


def level_of(rng, extent, cuts, low, largest):
    def one(position, blocks):
        draws = jax.random.uniform(jax.random.fold_in(jax.random.fold_in(rng, 6), position), (blocks,), jnp.float32, low / len(cuts), largest / len(cuts))
        return jnp.repeat(jnp.exp(draws), extent[position] // blocks).reshape((-1,) + (1,) * (len(extent) - position - 1))

    factor_of = one(*cuts[0])
    for cut in cuts[1:]:
        factor_of = factor_of * one(*cut)
    return factor_of


def scatter_about(own_key, extent, scale, limit, split=(), dtype=jnp.bfloat16):
    entries = scale * jax.random.normal(own_key, extent, jnp.float32)
    if split:
        entries = entries * level_of(own_key, extent, split, -0.22, 0.18)
    return jnp.clip(entries, -limit, limit).astype(dtype)


def setup_inputs(seed: int = 0) -> dict:
    seeds = jax.random.split(jax.random.key(seed), 13)
    final_hidden = draw_final_hidden(jax.random.fold_in(seeds[12], 71), 0)
    value_head = draw_value_head(jax.random.fold_in(seeds[12], 71), 0)
    norm_gain = jnp.clip(1.0 + 0.1 * jax.random.normal(seeds[2], (D,), jnp.float32), 0.5, 1.5).astype(jnp.bfloat16)
    rewards = scatter_about(seeds[3], (TOKENS,), 0.5, 6.0, ((0, 32),), jnp.float32)
    old_values = scatter_about(seeds[4], (TOKENS,), 0.5, 6.0, ((0, 32),), jnp.float32)
    loss_mask = touch_ends((jax.random.randint(seeds[5], (TOKENS,), 0, 4) < 3).astype(jnp.int32), jax.random.fold_in(seeds[5], 1), 0, 1)
    row_exp = touch_ends(jax.random.randint(seeds[6], (GROUPS, D), -14, -10), jax.random.fold_in(seeds[6], 1), -14, (-10) - 1).astype(jnp.int32)
    gain_exp = touch_ends(jax.random.randint(seeds[7], (GROUPS, D // GBLK), -16, -6), jax.random.fold_in(seeds[7], 1), -16, (-6) - 1).astype(jnp.int32)
    first_w = scatter_about(seeds[8], (D, BINS), 0.3, 4.0, ((0, 32),), jnp.float32)
    second_w = jnp.clip(jnp.exp(math.log(1.0) - 4.6051702 * jax.random.uniform(seeds[9], (D, BINS), jnp.float32) ** level_of(seeds[9], (D, BINS), ((0, 32),), -0.2, 0.2)), 0.01, 1.0)
    first_g = scatter_about(seeds[10], (D,), 0.3, 4.0, ((0, 32),), jnp.float32)
    second_g = jnp.clip(jnp.exp(math.log(1.0) - 4.6051702 * jax.random.uniform(seeds[11], (D,), jnp.float32) ** level_of(seeds[11], (D,), ((0, 32),), -0.2, 0.2)), 0.01, 1.0)
    return {"final_hidden": final_hidden, "value_head": value_head, "norm_gain": norm_gain, "rewards": rewards, "old_values": old_values, "loss_mask": loss_mask, "row_exp": row_exp, "gain_exp": gain_exp, "first_w": first_w, "second_w": second_w, "first_g": first_g, "second_g": second_g}


LOGIT_SCALE = 0.0625
RETURN_LOW = -4.0
RETURN_HIGH = 4.0
TRACE_DECAY = 0.95
SAT_LIMIT = 448.0
LEARN_RATE = 0.02
FIRST_CORR = 0.19
SECOND_CORR = 0.0975
EPSILON = 1e-08
NORM_EPSILON = 1e-06

def gauss_targets(returns):
    width = (RETURN_HIGH - RETURN_LOW) / BINS
    spread = 0.75 * width
    bin_edges = RETURN_LOW + width * jnp.arange(BINS + 1).astype(jnp.float32)
    clamped = jnp.clip(returns, RETURN_LOW, RETURN_HIGH)
    cum_mass = 0.5 * (1.0 + jax.scipy.special.erf((bin_edges[None, :] - clamped[:, None]) / (spread * math.sqrt(2.0))))
    bin_mass = cum_mass[:, 1:] - cum_mass[:, :-1]
    return bin_mass / (cum_mass[:, -1:] - cum_mass[:, :1])

def gae_returns(rewards, old_values):
    reward_rows = rewards.reshape(-1, SEQ)
    value_rows = old_values.reshape(-1, SEQ)
    following = jnp.concatenate([value_rows[:, 1:], jnp.zeros((value_rows.shape[0], 1), jnp.float32)], axis=1)
    td_error = reward_rows + following - value_rows

    def backward(carry, column):
        carry = column + TRACE_DECAY * carry
        return (carry, carry)
    final_carry, traced = lax.scan(backward, jnp.zeros((value_rows.shape[0],), jnp.float32), td_error.T, reverse=True)
    return (traced.T + value_rows).reshape(-1)

def local_terms(hidden, gain, head, targets, mask, row_scale_exp, block_scale_exp):
    hidden_f = hidden.astype(jnp.float32)
    inv_rms = lax.rsqrt(lax.optimization_barrier(jnp.mean(hidden_f * hidden_f, axis=1, keepdims=True)) + NORM_EPSILON)
    normed = hidden_f * inv_rms
    scaled = (normed * gain.astype(jnp.float32)).astype(jnp.bfloat16)
    logits = LOGIT_SCALE * jnp.dot(scaled, head, preferred_element_type=jnp.float32)
    shifted = jnp.exp(logits - lax.optimization_barrier(jnp.max(logits, axis=1, keepdims=True)))
    probs_out = shifted / lax.optimization_barrier(jnp.sum(shifted, axis=1, keepdims=True))
    errors = (LOGIT_SCALE * mask.astype(jnp.float32)[:, None] * (probs_out - targets)).astype(jnp.bfloat16)
    weight_part = lax.dot_general(scaled, errors, (((0,), (0,)), ((), ())), preferred_element_type=jnp.float32)
    back_prop = lax.dot_general(errors, head, (((1,), (1,)), ((), ())), preferred_element_type=jnp.float32)
    gain_part = lax.optimization_barrier(jnp.sum(back_prop * normed, axis=0))
    row_limit = SAT_LIMIT * jnp.exp2(row_scale_exp.astype(jnp.float32))
    block_limit = SAT_LIMIT * jnp.repeat(jnp.exp2(block_scale_exp.astype(jnp.float32)), GBLK)
    weight_q = jnp.clip(weight_part, -row_limit[:, None], row_limit[:, None]).astype(jnp.bfloat16)
    gain_q = jnp.clip(gain_part, -block_limit, block_limit).astype(jnp.bfloat16)
    return lax.optimization_barrier((weight_q, gain_q))

def adam_update(param, grad, first, second):
    first_new = 0.9 * first + 0.1 * grad
    second_new = 0.95 * second + 0.05 * grad * grad
    update = first_new / FIRST_CORR / (jnp.sqrt(second_new / SECOND_CORR) + EPSILON)
    return ((param.astype(jnp.float32) - LEARN_RATE * update).astype(jnp.bfloat16), first_new, second_new)

def reference(final_hidden, value_head, norm_gain, rewards, old_values, loss_mask, row_exp, gain_exp, first_w, second_w, first_g, second_g):
    group_count = N_DP * N_NODE * N_PIPE
    targets = gauss_targets(gae_returns(rewards, old_values))

    def add_group(carry, group):
        start = group * T_DEV
        hidden = lax.dynamic_slice_in_dim(final_hidden, start, T_DEV, 0)
        group_targets = lax.dynamic_slice_in_dim(targets, start, T_DEV, 0)
        group_mask = lax.dynamic_slice_in_dim(loss_mask, start, T_DEV, 0)
        row_scale_exp = lax.dynamic_slice_in_dim(row_exp, group, 1, 0)[0]
        block_scale_exp = lax.dynamic_slice_in_dim(gain_exp, group, 1, 0)[0]
        weight_q, gain_q = local_terms(hidden, norm_gain, value_head, group_targets, group_mask, row_scale_exp, block_scale_exp)
        return ((carry[0] + weight_q.astype(jnp.float32), carry[1] + gain_q.astype(jnp.float32)), None)
    initial = (jnp.zeros((D, BINS), jnp.float32), jnp.zeros((D,), jnp.float32))
    totals, unused = lax.scan(add_group, initial, jnp.arange(group_count).astype(jnp.int32))
    new_weight, first_w_new, second_w_new = adam_update(value_head, totals[0], first_w, second_w)
    new_gain, first_g_new, second_g_new = adam_update(norm_gain, totals[1], first_g, second_g)
    return (new_weight, new_gain, first_w_new, second_w_new, first_g_new, second_g_new)
```

```python
import functools
import math

import jax
import jax.numpy as jnp
from jax import lax
from jax.experimental import pallas as pl
from jax.experimental.pallas import tpu as pltpu
from jax.sharding import PartitionSpec as P

BINS = 128
GBLK = 128
SEQ = 32


LOGIT_SCALE = 0.0625
RETURN_LOW = -4.0
RETURN_HIGH = 4.0
TRACE_DECAY = 0.95
SAT_LIMIT = 448.0
LEARN_RATE = 0.02
FIRST_CORR = 0.19
SECOND_CORR = 0.0975
EPSILON = 1e-08
NORM_EPSILON = 1e-06


def gauss_targets(returns):
    width = (RETURN_HIGH - RETURN_LOW) / BINS
    spread = 0.75 * width
    bin_edges = RETURN_LOW + width * jnp.arange(BINS + 1).astype(jnp.float32)
    clamped = jnp.clip(returns, RETURN_LOW, RETURN_HIGH)
    cum_mass = 0.5 * (
        1.0
        + jax.scipy.special.erf((bin_edges[None, :] - clamped[:, None]) / (spread * math.sqrt(2.0)))
    )
    bin_mass = cum_mass[:, 1:] - cum_mass[:, :-1]
    return bin_mass / (cum_mass[:, -1:] - cum_mass[:, :1])


def gae_returns(rewards, old_values):
    reward_rows = rewards.reshape(-1, SEQ)
    value_rows = old_values.reshape(-1, SEQ)
    following = jnp.concatenate(
        [value_rows[:, 1:], jnp.zeros((value_rows.shape[0], 1), jnp.float32)], axis=1
    )
    td_error = reward_rows + following - value_rows
    row_pos = lax.broadcasted_iota(jnp.int32, (SEQ, SEQ), 0)
    col_pos = lax.broadcasted_iota(jnp.int32, (SEQ, SEQ), 1)
    offset = jnp.maximum(row_pos - col_pos, 0).astype(jnp.float32)
    kernel = jnp.where(row_pos >= col_pos, jnp.power(TRACE_DECAY, offset), 0.0)
    traced = jnp.dot(td_error, kernel, precision=lax.Precision.HIGHEST)
    return (traced + value_rows).reshape(-1)


def local_terms(hidden, gain, head, targets, mask, row_scale_exp, block_scale_exp):
    hidden_f = hidden.astype(jnp.float32)
    inv_rms = lax.rsqrt(jnp.mean(hidden_f * hidden_f, axis=1, keepdims=True) + NORM_EPSILON)
    normed = hidden_f * inv_rms
    scaled = (normed * gain.astype(jnp.float32)).astype(jnp.bfloat16)
    logits = LOGIT_SCALE * jnp.dot(scaled, head, preferred_element_type=jnp.float32)
    shifted = jnp.exp(logits - jnp.max(logits, axis=1, keepdims=True))
    probs_out = shifted / jnp.sum(shifted, axis=1, keepdims=True)
    errors = (LOGIT_SCALE * mask.astype(jnp.float32)[:, None] * (probs_out - targets)).astype(
        jnp.bfloat16
    )
    row_limit = SAT_LIMIT * jnp.exp2(row_scale_exp.astype(jnp.float32))
    block_limit = SAT_LIMIT * jnp.repeat(jnp.exp2(block_scale_exp.astype(jnp.float32)), GBLK)
    return inv_rms, errors, row_limit[None, :], block_limit[None, :]


def adam_update(param, grad, first, second):
    first_new = 0.9 * first + 0.1 * grad
    second_new = 0.95 * second + 0.05 * grad * grad
    update = first_new / FIRST_CORR / (jnp.sqrt(second_new / SECOND_CORR) + EPSILON)
    return (
        (param.astype(jnp.float32) - LEARN_RATE * update).astype(jnp.bfloat16),
        first_new,
        second_new,
    )


LANES = 128
GAIN_ROWS = 16
VMEM_GRANT = 40000000
MESH = pl.DeviceIdType.MESH


def far_first(size):
    ring = [min(step, size - step) for step in range(size)]
    return sorted(range(size), key=lambda step: -ring[step])


def exchange(
    sizes,
    rows,
    hidden,
    inv_rms,
    errors_in,
    head,
    gain,
    row_limit,
    gain_limit,
    gain_blocks,
    first_w,
    second_w,
    first_g,
    second_g,
    new_weight,
    new_gain,
    first_w_new,
    second_w_new,
    first_g_new,
    second_g_new,
    quant,
    dp_buf,
    part,
    node_buf,
    pipe_out,
    pipe_buf,
    shared,
    dp_send,
    dp_recv,
    node_send,
    node_recv,
    pipe_send,
    pipe_recv,
    all_send,
    all_recv,
):
    n_dp, n_node, n_pipe = sizes
    me_dp = lax.axis_index("dp")
    me_node = lax.axis_index("node")
    me_pipe = lax.axis_index("pipe")
    gain_rows = first_g.shape[0]

    barrier = pltpu.get_barrier_semaphore()
    for axis, size, me in (("dp", n_dp, me_dp), ("node", n_node, me_node), ("pipe", n_pipe, me_pipe)):
        for step in range(1, size):
            pl.semaphore_signal(
                barrier, inc=1, device_id={axis: lax.rem(me + step, size)}, device_id_type=MESH
            )
    pl.semaphore_wait(barrier, n_dp + n_node + n_pipe - 3)

    order = far_first(n_pipe)

    def dp_copy(chunk, step):
        peer = lax.rem(me_dp + step, n_dp)
        return pltpu.make_async_remote_copy(
            src_ref=quant.at[peer, lax.rem(me_pipe + order[chunk], n_pipe)],
            dst_ref=dp_buf.at[step - 1, chunk],
            send_sem=dp_send.at[step - 1, chunk],
            recv_sem=dp_recv.at[step - 1, chunk],
            device_id={"dp": peer},
            device_id_type=MESH,
        )

    def node_copy(chunk, step):
        peer = lax.rem(me_node + step, n_node)
        return pltpu.make_async_remote_copy(
            src_ref=part.at[chunk, peer],
            dst_ref=node_buf.at[step - 1, chunk],
            send_sem=node_send.at[step - 1, chunk],
            recv_sem=node_recv.at[step - 1, chunk],
            device_id={"node": peer},
            device_id_type=MESH,
        )

    def pipe_copy(chunk):
        return pltpu.make_async_remote_copy(
            src_ref=pipe_out.at[chunk],
            dst_ref=pipe_buf.at[chunk],
            send_sem=pipe_send.at[chunk],
            recv_sem=pipe_recv.at[chunk],
            device_id={"pipe": lax.rem(me_pipe + order[chunk], n_pipe)},
            device_id_type=MESH,
        )

    def all_copy(step):
        return pltpu.make_async_remote_copy(
            src_ref=shared.at[me_pipe],
            dst_ref=shared.at[me_pipe],
            send_sem=all_send.at[step - 1],
            recv_sem=all_recv.at[step - 1],
            device_id={"pipe": lax.rem(me_pipe + step, n_pipe)},
            device_id_type=MESH,
        )

    tokens = hidden.shape[0]
    pad_rows = quant.shape[3] - rows
    errors = errors_in[...]
    errors_t = errors.astype(jnp.float32).T.astype(jnp.bfloat16)
    inverse = jnp.broadcast_to(inv_rms[...], (tokens, LANES))
    pad_index = lax.broadcasted_iota(jnp.int32, (pad_rows, LANES), 0)

    def multiply(dp, node, first_pipe, count):
        width = count * rows
        start = pl.multiple_of(((dp * n_node + node) * n_pipe + first_pipe) * rows, width)
        columns = pl.ds(start, width)
        normed = hidden[:, columns].astype(jnp.float32) * jnp.tile(inverse, (1, width // LANES))
        scaled = (normed * gain[:, columns]).astype(jnp.bfloat16)
        weight_t = jnp.dot(errors_t, scaled, preferred_element_type=jnp.float32)
        limit = row_limit[:, columns]
        weight = jnp.clip(weight_t, -limit, limit).T.astype(jnp.bfloat16)
        back_prop = lax.dot_general(
            errors, head[columns, :], (((1,), (1,)), ((), ())), preferred_element_type=jnp.float32
        )
        gain_part = jnp.sum(back_prop * normed, axis=0, keepdims=True)
        limit = gain_limit[:, columns]
        gain_part = jnp.clip(gain_part, -limit, limit)
        for index in range(count):
            pipe = first_pipe + index
            quant[dp, pipe, node, 0:rows] = weight[index * rows : (index + 1) * rows]
            padded = jnp.zeros((pad_rows, LANES), jnp.float32)
            for row in range(gain_rows):
                low = index * rows + row * LANES
                taken = min(LANES, rows - row * LANES)
                line = gain_part[:, low : low + taken]
                if taken < LANES:
                    line = jnp.concatenate([line, jnp.zeros((1, LANES - taken), jnp.float32)], axis=1)
                padded = jnp.where(pad_index == row, line, padded)
            quant[dp, pipe, node, rows : rows + pad_rows] = padded.astype(jnp.bfloat16)

    aligned = rows % LANES == 0

    def multiply_chunk(step, chunk):
        dp = lax.rem(me_dp + step, n_dp)
        if aligned:
            pipe = lax.rem(me_pipe + order[chunk], n_pipe)
            lax.fori_loop(0, n_node, lambda node, _: (multiply(dp, node, pipe, 1), _)[1], 0)
        elif chunk == 0:
            lax.fori_loop(0, n_node, lambda node, _: (multiply(dp, node, 0, n_pipe), _)[1], 0)

    for chunk in range(n_pipe):
        for step in range(1, n_dp):
            multiply_chunk(step, chunk)
            dp_copy(chunk, step).start()

    def dp_sum(chunk):
        own = lax.rem(me_pipe + order[chunk], n_pipe)
        multiply_chunk(0, chunk)
        for step in range(1, n_dp):
            dp_copy(chunk, step).wait_recv()
        for away in range(1, n_node + 1):
            node = lax.rem(me_node + away, n_node)
            total = quant[me_dp, own, node].astype(jnp.float32)
            for step in range(1, n_dp):
                total = total + dp_buf[step - 1, chunk, node].astype(jnp.float32)
            part[chunk, node] = total.astype(jnp.bfloat16)
            if away < n_node:
                node_copy(chunk, away).start()

    def node_sum(chunk):
        for step in range(1, n_node):
            node_copy(chunk, step).wait_recv()
        total = part[chunk, me_node].astype(jnp.float32)
        for step in range(1, n_node):
            total = total + node_buf[step - 1, chunk].astype(jnp.float32)
        pipe_out[chunk] = total.astype(jnp.bfloat16)
        if order[chunk] != 0:
            pipe_copy(chunk).start()

    for chunk in range(n_pipe):
        dp_sum(chunk)
        if chunk >= 1:
            node_sum(chunk - 1)
    node_sum(n_pipe - 1)

    for chunk in range(n_pipe - 1):
        pipe_copy(chunk).wait_recv()

    def adam(start, count, param, first, second, first_out, second_out):
        grad = pipe_out[n_pipe - 1, start : start + count].astype(jnp.float32)
        for chunk in range(n_pipe - 1):
            grad = grad + pipe_buf[chunk, start : start + count].astype(jnp.float32)
        new, first_new, second_new = adam_update(param, grad, first[...], second[...])
        first_out[...] = first_new
        second_out[...] = second_new
        return new

    position = (me_dp * n_node + me_node) * n_pipe + me_pipe
    own_weight = head[pl.ds(pl.multiple_of(position * rows, rows), rows), :]
    shared[me_pipe, rows : rows + gain_rows] = adam(
        rows, gain_rows, gain_blocks[position], first_g, second_g, first_g_new, second_g_new
    )
    shared[me_pipe, 0:rows] = adam(
        0, rows, own_weight, first_w, second_w, first_w_new, second_w_new
    )
    for step in range(1, n_pipe):
        all_copy(step).start()
    for chunk in range(n_pipe):
        for step in range(1, n_dp):
            dp_copy(chunk, step).wait_send()
        for step in range(1, n_node):
            node_copy(chunk, step).wait_send()
        if order[chunk] != 0:
            pipe_copy(chunk).wait_send()
    for step in range(1, n_pipe):
        all_copy(step).wait()
    for pipe in range(n_pipe):
        new_weight[pipe] = shared[pipe, 0:rows]
        new_gain[pipe] = shared[pipe, rows : rows + gain_rows]


def write_out(*refs):
    half = len(refs) // 2
    for source, target in zip(refs[:half], refs[half:]):
        target[...] = source[...]


def shards(
    final_hidden,
    value_head,
    norm_gain,
    rewards,
    old_values,
    loss_mask,
    row_exp,
    gain_exp,
    first_w,
    second_w,
    first_g,
    second_g,
):
    targets = gauss_targets(gae_returns(rewards, old_values))
    inv_rms, errors, row_limit, gain_limit = local_terms(
        final_hidden, norm_gain, value_head, targets, loss_mask, row_exp[0], gain_exp[0]
    )
    sizes = tuple(lax.axis_size(axis) for axis in ("dp", "node", "pipe"))
    n_dp, n_node, n_pipe = sizes
    rows = first_g.shape[0]
    bins = value_head.shape[1]
    gain_rows = -(-rows // bins)
    block_rows = rows + -(-gain_rows // GAIN_ROWS) * GAIN_ROWS

    def to_rows(values, total):
        lead = values.shape[:-1]
        values = jnp.pad(values, [(0, 0)] * len(lead) + [(0, total * bins - rows)])
        return values.reshape(lead + (total, bins))

    block = (block_rows, bins)
    vmem = pl.BlockSpec(memory_space=pltpu.VMEM)
    f32 = jnp.float32
    bf16 = jnp.bfloat16
    shapes = (
        jax.ShapeDtypeStruct((n_pipe, rows, bins), bf16),
        jax.ShapeDtypeStruct((n_pipe, gain_rows, bins), bf16),
        jax.ShapeDtypeStruct((rows, bins), f32),
        jax.ShapeDtypeStruct((rows, bins), f32),
        jax.ShapeDtypeStruct((gain_rows, bins), f32),
        jax.ShapeDtypeStruct((gain_rows, bins), f32),
    )
    buffers = [
        (n_dp, n_pipe, n_node) + block,
        (n_dp - 1, n_pipe, n_node) + block,
        (n_pipe, n_node) + block,
        (n_node - 1, n_pipe) + block,
        (n_pipe,) + block,
        (n_pipe,) + block,
        (n_pipe,) + block,
    ]
    held = 2 * sum(math.prod(shape) for shape in buffers)
    held += 2 * (final_hidden.size + value_head.size) + 24 * rows * bins
    updated = pl.pallas_call(
        functools.partial(exchange, sizes, rows),
        out_shape=shapes,
        in_specs=[vmem] * 12,
        out_specs=(vmem,) * 6,
        scratch_shapes=[pltpu.VMEM(shape, bf16) for shape in buffers]
        + [
            pltpu.SemaphoreType.DMA((n_dp - 1, n_pipe)),
            pltpu.SemaphoreType.DMA((n_dp - 1, n_pipe)),
            pltpu.SemaphoreType.DMA((n_node - 1, n_pipe)),
            pltpu.SemaphoreType.DMA((n_node - 1, n_pipe)),
            pltpu.SemaphoreType.DMA((n_pipe,)),
            pltpu.SemaphoreType.DMA((n_pipe,)),
            pltpu.SemaphoreType.DMA((n_pipe - 1,)),
            pltpu.SemaphoreType.DMA((n_pipe - 1,)),
        ],
        compiler_params=pltpu.CompilerParams(
            collective_id=0, has_side_effects=True, vmem_limit_bytes=held + (12 << 20)
        ),
    )(
        final_hidden,
        inv_rms,
        errors,
        value_head,
        norm_gain.astype(f32)[None, :],
        row_limit,
        gain_limit,
        to_rows(norm_gain.reshape(-1, rows), gain_rows),
        first_w,
        second_w,
        to_rows(first_g, gain_rows),
        to_rows(second_g, gain_rows),
    )
    new_weight, new_gain, first_w_new, second_w_new, first_g_new, second_g_new = pl.pallas_call(
        write_out,
        out_shape=shapes,
        in_specs=[vmem] * 6,
        out_specs=(vmem,) * 6,
        compiler_params=pltpu.CompilerParams(vmem_limit_bytes=8 << 20),
    )(*updated)

    def from_rows(values):
        lead = values.shape[:-2]
        return values.reshape(lead + (gain_rows * bins,))[..., :rows].reshape(-1)

    return (
        new_weight.reshape(n_pipe * rows, bins),
        from_rows(new_gain),
        first_w_new,
        second_w_new,
        from_rows(first_g_new),
        from_rows(second_g_new),
    )


def ahead(n_pipe, me_pipe, step):
    return lax.rem(me_pipe + step, n_pipe)


def fused(
    sizes,
    rows,
    hidden_in,
    head_in,
    gain_in,
    rewards_in,
    values_in,
    mask_in,
    row_exp_in,
    gain_exp_in,
    first_w_in,
    second_w_in,
    first_g_in,
    second_g_in,
    new_weight,
    new_gain,
    first_w_new,
    second_w_new,
    first_g_new,
    second_g_new,
    hidden,
    head,
    gain_raw,
    rewards,
    values,
    mask,
    row_exp,
    gain_exp,
    first_w,
    second_w,
    first_g,
    second_g,
    gain,
    row_limit,
    gain_limit,
    quant,
    dp_buf,
    part,
    near_buf,
    far_out,
    far_buf,
    held,
    pipe_out,
    pipe_buf,
    own,
    gain_quant,
    gain_dp,
    gain_part,
    gain_node,
    gain_sum,
    gain_pipe,
    gain_all,
    load_sem,
    hidden_sem,
    head_sem,
    dp_send,
    dp_recv,
    near_send,
    near_recv,
    far_send,
    far_recv,
    pipe_send,
    pipe_recv,
    all_send,
    all_recv,
    gain_send,
    gain_recv,
):
    n_dp, n_node, n_pipe = sizes
    me_dp = lax.axis_index("dp")
    me_node = lax.axis_index("node")
    me_pipe = lax.axis_index("pipe")
    me_high, me_low = me_node // 2, lax.rem(me_node, 2)
    f32, bf16 = jnp.float32, jnp.bfloat16
    halves = rows // LANES
    tokens, width = hidden.shape
    bins = head.shape[1]
    chunks = hidden_sem.shape[0]
    step_width = width // chunks
    peer_dp = 1 - me_dp

    small = (
        (rewards_in, rewards),
        (values_in, values),
        (mask_in, mask),
        (gain_in, gain_raw),
        (row_exp_in, row_exp),
        (gain_exp_in, gain_exp),
        (first_w_in, first_w),
        (second_w_in, second_w),
        (first_g_in, first_g),
        (second_g_in, second_g),
    )
    loads = [pltpu.make_async_copy(*pair, load_sem.at[index]) for index, pair in enumerate(small)]
    hidden_loads = []
    head_loads = []
    for chunk in range(chunks):
        span = pl.ds(chunk * step_width, step_width)
        hidden_loads.append(
            pltpu.make_async_copy(hidden_in.at[:, span], hidden.at[:, span], hidden_sem.at[chunk])
        )
        head_loads.append(
            pltpu.make_async_copy(head_in.at[span, :], head.at[span, :], head_sem.at[chunk])
        )
    for copy in loads[:4]:
        copy.start()
    for chunk in range(chunks):
        hidden_loads[chunk].start()
        head_loads[chunk].start()
    for copy in loads[4:]:
        copy.start()

    barrier = pltpu.get_barrier_semaphore()
    for axis, size, me in (("dp", n_dp, me_dp), ("node", n_node, me_node), ("pipe", n_pipe, me_pipe)):
        for step in range(1, size):
            pl.semaphore_signal(
                barrier, inc=1, device_id={axis: lax.rem(me + step, size)}, device_id_type=MESH
            )

    for copy in loads[:4]:
        copy.wait()
    at = lax.broadcasted_iota(jnp.int32, (tokens, tokens), 0)
    later = lax.broadcasted_iota(jnp.int32, (tokens, tokens), 1)
    reach = jnp.where(at // SEQ == later // SEQ, later - at, -1)
    decay = jnp.exp(jnp.maximum(reach, 0).astype(f32) * math.log(TRACE_DECAY))
    reward_part = jnp.where(reach >= 0, decay, 0.0) * rewards[...]
    value_part = jnp.where(reach > 0, decay * ((1.0 - TRACE_DECAY) / TRACE_DECAY), 0.0) * values[...]
    returns = jnp.sum(reward_part + value_part, axis=1, keepdims=True)
    returns = jnp.clip(returns, RETURN_LOW, RETURN_HIGH)
    counted = jnp.sum(
        jnp.where(at == later, mask[...].astype(f32), 0.0), axis=1, keepdims=True
    )
    bin_width = (RETURN_HIGH - RETURN_LOW) / bins
    sharp = 1.0 / (0.75 * bin_width * math.sqrt(2.0))
    edge = lax.broadcasted_iota(jnp.int32, (tokens, bins), 1).astype(f32) * bin_width + RETURN_LOW
    low_mass = lax.erf((edge - returns) * sharp)
    high_mass = lax.erf((edge + bin_width - returns) * sharp)
    targets = (high_mass - low_mass) / (high_mass[:, bins - 1 :] - low_mass[:, :1])
    gain[...] = gain_raw[...].astype(f32)

    groups = step_width // LANES
    squares = jnp.zeros((tokens, LANES), f32)
    logits = jnp.zeros((tokens, bins), f32)
    for chunk in range(chunks):
        hidden_loads[chunk].wait()
        head_loads[chunk].wait()
        pieces = []
        for group in range(groups):
            low = chunk * step_width + group * LANES
            piece = hidden[:, low : low + LANES].astype(f32)
            squares = squares + piece * piece
            line = low // LANES
            pieces.append((piece * gain[line : line + 1, :]).astype(bf16))
        logits = logits + jnp.dot(
            jnp.concatenate(pieces, axis=1),
            head[chunk * step_width : (chunk + 1) * step_width, :],
            preferred_element_type=f32,
        )
    for copy in loads[4:]:
        copy.wait()
    row_limit[...] = SAT_LIMIT * jnp.exp2(row_exp[...].astype(f32))
    lines = gain.shape[0]
    line_at = lax.broadcasted_iota(jnp.int32, (lines, lines), 0)
    line_of = lax.broadcasted_iota(jnp.int32, (lines, lines), 1)
    block_limit = SAT_LIMIT * jnp.exp2(gain_exp[...].astype(f32))
    block_limit = jnp.sum(jnp.where(line_at == line_of, block_limit, 0.0), axis=1, keepdims=True)
    gain_limit[...] = jnp.broadcast_to(block_limit, (lines, LANES))

    mean_square = jnp.sum(squares, axis=1, keepdims=True) * (1.0 / width)
    inv_rms = lax.rsqrt(mean_square + NORM_EPSILON)
    logits = logits * (inv_rms * LOGIT_SCALE)
    shifted = jnp.exp(logits - jnp.max(logits, axis=1, keepdims=True))
    probs = shifted / jnp.sum(shifted, axis=1, keepdims=True)
    scaled_errors = (counted * inv_rms * LOGIT_SCALE) * (probs - targets)
    errors = scaled_errors.astype(bf16)
    errors_t = scaled_errors.T.astype(bf16)

    pl.semaphore_wait(barrier, n_dp + n_node + n_pipe - 3)

    order = far_first(n_pipe)
    phases = [(half, slot) for half in range(halves) for slot in range(n_pipe)]

    def remote(source, target, send, recv, device_id):
        return pltpu.make_async_remote_copy(
            src_ref=source,
            dst_ref=target,
            send_sem=send,
            recv_sem=recv,
            device_id=device_id,
            device_id_type=MESH,
        )

    def dp_copy(half, slot):
        return remote(
            quant.at[peer_dp, half, slot],
            dp_buf.at[half, slot],
            dp_send.at[half, slot],
            dp_recv.at[half, slot],
            {"dp": peer_dp},
        )

    def low_first(slot):
        return slot % 2 == 0

    def low_peer():
        return me_high * 2 + 1 - me_low

    def high_peer():
        return (1 - me_high) * 2 + me_low

    def near_copy(half, slot):
        if low_first(slot):
            source, peer = part.at[half, slot, :, 1 - me_low], low_peer()
        else:
            source, peer = part.at[half, slot, 1 - me_high], high_peer()
        return remote(
            source,
            near_buf.at[half, slot],
            near_send.at[half, slot],
            near_recv.at[half, slot],
            {"node": peer},
        )

    def far_copy(half, slot):
        return remote(
            far_out.at[half, slot],
            far_buf.at[half, slot],
            far_send.at[half, slot],
            far_recv.at[half, slot],
            {"node": high_peer() if low_first(slot) else low_peer()},
        )

    def pipe_copy(half, slot):
        return remote(
            pipe_out.at[half, slot],
            pipe_buf.at[half, slot],
            pipe_send.at[half, slot],
            pipe_recv.at[half, slot],
            {"pipe": ahead(n_pipe, me_pipe, order[slot])},
        )

    def all_copy(half, slot):
        return remote(
            new_weight.at[me_pipe, half],
            new_weight.at[me_pipe, half],
            all_send.at[half, slot],
            all_recv.at[half, slot],
            {"pipe": ahead(n_pipe, me_pipe, order[slot])},
        )

    def gain_copy(source, target, index, device_id):
        return remote(source, target, gain_send.at[index], gain_recv.at[index], device_id)

    gain_dp_copy = gain_copy(gain_quant.at[peer_dp], gain_dp, 0, {"dp": peer_dp})
    gain_node_copies = []
    for step in range(1, n_node):
        peer = lax.rem(me_node + step, n_node)
        gain_node_copies.append(
            gain_copy(gain_part.at[peer], gain_node.at[step - 1], step, {"node": peer})
        )
    gain_pipe_copies = []
    gain_all_copies = []
    for step in range(1, n_pipe):
        peer = ahead(n_pipe, me_pipe, step)
        gain_pipe_copies.append(
            gain_copy(
                gain_sum.at[peer], gain_pipe.at[step - 1], n_node + step - 1, {"pipe": peer}
            )
        )
        gain_all_copies.append(
            gain_copy(
                gain_all.at[me_pipe],
                gain_all.at[me_pipe],
                n_node + n_pipe + step - 2,
                {"pipe": peer},
            )
        )

    def multiply(dp, slot):
        pipe = ahead(n_pipe, me_pipe, order[slot])
        for node in range(n_node):
            block = (dp * n_node + node) * n_pipe + pipe
            span = pl.ds(pl.multiple_of(block * rows, rows), rows)
            columns = hidden[:, span]
            weight_t = jnp.dot(errors_t, columns, preferred_element_type=f32)
            back_prop = lax.dot_general(
                errors, head[span, :], (((1,), (1,)), ((), ())), preferred_element_type=f32
            )
            gain_line = jnp.sum(back_prop * columns.astype(f32), axis=0, keepdims=True)
            for half in range(halves):
                line = pl.ds(block * halves + half, 1)
                low = half * LANES
                limit = row_limit[line, :]
                weight = weight_t[:, low : low + LANES] * gain[line, :]
                quant[dp, half, slot, node // 2, node % 2] = jnp.clip(
                    weight, -limit, limit
                ).astype(bf16)
                limit = gain_limit[line, :]
                taken = jnp.clip(gain_line[:, low : low + LANES], -limit, limit)
                gain_quant[dp, node, pipe, half] = taken.astype(bf16).astype(f32)

    def add_dp(half, slot):
        dp_copy(half, slot).wait_recv()
        total = quant[me_dp, half, slot].astype(f32) + dp_buf[half, slot].astype(f32)
        part[half, slot] = total.astype(bf16)
        near_copy(half, slot).start()

    def add_near(half, slot):
        near_copy(half, slot).wait_recv()
        if low_first(slot):
            sent, kept = part[half, slot, 1 - me_high, me_low], part[half, slot, me_high, me_low]
            other, mine = 1 - me_high, me_high
        else:
            sent, kept = part[half, slot, me_high, 1 - me_low], part[half, slot, me_high, me_low]
            other, mine = 1 - me_low, me_low
        total = sent.astype(f32) + near_buf[half, slot, other].astype(f32)
        far_out[half, slot] = total.astype(bf16)
        far_copy(half, slot).start()
        held[half, slot] = kept.astype(f32) + near_buf[half, slot, mine].astype(f32)

    def add_far(half, slot):
        far_copy(half, slot).wait_recv()
        total = held[half, slot] + far_buf[half, slot].astype(f32)
        if order[slot] == 0:
            own[half] = total
        else:
            pipe_out[half, slot] = total.astype(bf16)
            pipe_copy(half, slot).start()

    position = (me_dp * n_node + me_node) * n_pipe + me_pipe

    def finish(half):
        total = own[half]
        for slot in range(n_pipe):
            if order[slot] != 0:
                pipe_copy(half, slot).wait_recv()
                total = total + pipe_buf[half, slot].astype(f32)
        low = half * LANES
        start = pl.multiple_of(position * rows + low, LANES)
        new, first, second = adam_update(
            head[pl.ds(start, LANES), :],
            total.T,
            first_w[low : low + LANES, :],
            second_w[low : low + LANES, :],
        )
        new_weight[me_pipe, half] = new
        for slot in range(n_pipe):
            if order[slot] != 0:
                all_copy(half, slot).start()
        first_w_new[low : low + LANES, :] = first
        second_w_new[low : low + LANES, :] = second

    def gain_add_dp():
        gain_dp_copy.wait_recv()
        gain_part[...] = gain_quant[me_dp] + gain_dp[...]
        for copy in gain_node_copies:
            copy.start()

    def gain_add_node():
        total = gain_part[me_node]
        for index, copy in enumerate(gain_node_copies):
            copy.wait_recv()
            total = total + gain_node[index]
        gain_sum[...] = total
        for copy in gain_pipe_copies:
            copy.start()

    def gain_finish():
        total = gain_sum[me_pipe]
        for index, copy in enumerate(gain_pipe_copies):
            copy.wait_recv()
            total = total + gain_pipe[index]
        for half in range(halves):
            param = gain[pl.ds(position * halves + half, 1), :]
            new, first, second = adam_update(param, total[half], first_g[half], second_g[half])
            gain_all[me_pipe, half] = new.astype(f32)
            first_g_new[half] = first
            second_g_new[half] = second
        for copy in gain_all_copies:
            copy.start()

    for slot in range(n_pipe):
        multiply(peer_dp, slot)
        for half in range(halves):
            dp_copy(half, slot).start()
    gain_dp_copy.start()
    count = len(phases)

    def advance(index):
        if index < count:
            add_dp(*phases[index])
        if 0 <= index - 2 < count:
            add_near(*phases[index - 2])
        if 0 <= index - 3 < count:
            add_far(*phases[index - 3])
        for half in range(halves - 1):
            if index - 3 == half * n_pipe + n_pipe + 1:
                finish(half)

    for slot in range(n_pipe):
        multiply(me_dp, slot)
        advance(slot)
    gain_add_dp()
    for index in range(n_pipe, count + 3):
        advance(index)
        if index == n_pipe:
            gain_add_node()
        if index == n_pipe + 2:
            gain_finish()
    finish(halves - 1)

    for half, slot in phases:
        dp_copy(half, slot).wait_send()
        near_copy(half, slot).wait_send()
        far_copy(half, slot).wait_send()
        if order[slot] != 0:
            pipe_copy(half, slot).wait_send()
    gain_dp_copy.wait_send()
    for copy in gain_node_copies + gain_pipe_copies:
        copy.wait_send()
    for copy in gain_all_copies:
        copy.wait()
    new_gain[...] = gain_all[...].reshape(n_pipe * halves, LANES).astype(bf16)
    for half, slot in phases:
        if order[slot] != 0:
            all_copy(half, slot).wait()


def send_home(*refs):
    count = (len(refs) - 1) // 2
    sems = refs[-1]
    copies = [
        pltpu.make_async_copy(refs[index], refs[count + index], sems.at[index])
        for index in range(count)
    ]
    for copy in copies:
        copy.start()
    for copy in copies:
        copy.wait()


def fused_shards(
    final_hidden,
    value_head,
    norm_gain,
    rewards,
    old_values,
    loss_mask,
    row_exp,
    gain_exp,
    first_w,
    second_w,
    first_g,
    second_g,
):
    sizes = tuple(lax.axis_size(axis) for axis in ("dp", "node", "pipe"))
    n_dp, n_node, n_pipe = sizes
    rows = first_g.shape[0]
    tokens, width = final_hidden.shape
    bins = value_head.shape[1]
    halves = rows // LANES
    lines = width // LANES
    chunks = max(1, width // 1024)
    f32, bf16, i32 = jnp.float32, jnp.bfloat16, jnp.int32
    vmem = pl.BlockSpec(memory_space=pltpu.VMEM)
    hbm = pl.BlockSpec(memory_space=pltpu.HBM)
    tile = (bins, LANES)
    shapes = (
        jax.ShapeDtypeStruct((n_pipe, halves, LANES, bins), bf16),
        jax.ShapeDtypeStruct((n_pipe * halves, LANES), bf16),
        jax.ShapeDtypeStruct((rows, bins), f32),
        jax.ShapeDtypeStruct((rows, bins), f32),
        jax.ShapeDtypeStruct((halves, 1, LANES), f32),
        jax.ShapeDtypeStruct((halves, 1, LANES), f32),
    )
    buffers = [
        ((tokens, width), bf16),
        ((width, bins), bf16),
        ((lines, LANES), bf16),
        ((1, tokens), f32),
        ((1, tokens), f32),
        ((1, tokens), i32),
        ((lines, LANES), i32),
        ((1, lines), i32),
        ((rows, bins), f32),
        ((rows, bins), f32),
        ((halves, 1, LANES), f32),
        ((halves, 1, LANES), f32),
        ((lines, LANES), f32),
        ((lines, LANES), f32),
        ((lines, LANES), f32),
        ((n_dp, halves, n_pipe, 2, 2) + tile, bf16),
        ((halves, n_pipe, 2, 2) + tile, bf16),
        ((halves, n_pipe, 2, 2) + tile, bf16),
        ((halves, n_pipe, 2) + tile, bf16),
        ((halves, n_pipe) + tile, bf16),
        ((halves, n_pipe) + tile, bf16),
        ((halves, n_pipe) + tile, f32),
        ((halves, n_pipe) + tile, bf16),
        ((halves, n_pipe) + tile, bf16),
        ((halves,) + tile, f32),
        ((n_dp, n_node, n_pipe, halves, 1, LANES), f32),
        ((n_node, n_pipe, halves, 1, LANES), f32),
        ((n_node, n_pipe, halves, 1, LANES), f32),
        ((n_node - 1, n_pipe, halves, 1, LANES), f32),
        ((n_pipe, halves, 1, LANES), f32),
        ((n_pipe - 1, halves, 1, LANES), f32),
        ((n_pipe, halves, 1, LANES), f32),
    ]
    dma = pltpu.SemaphoreType.DMA
    semaphores = [(10,), (chunks,), (chunks,)]
    semaphores += [(halves, n_pipe)] * 10
    semaphores += [(n_node + 2 * n_pipe - 2,)] * 2
    updated = pl.pallas_call(
        functools.partial(fused, sizes, rows),
        out_shape=shapes,
        in_specs=[hbm] * 12,
        out_specs=(vmem,) * 6,
        scratch_shapes=[pltpu.VMEM(shape, kind) for shape, kind in buffers]
        + [dma(shape) for shape in semaphores],
        compiler_params=pltpu.CompilerParams(
            collective_id=0, has_side_effects=True, vmem_limit_bytes=VMEM_GRANT
        ),
    )(
        *[pltpu.with_memory_space_constraint(value, pltpu.HBM) for value in (
        final_hidden,
        value_head,
        norm_gain.reshape(lines, LANES),
        rewards.reshape(1, tokens),
        old_values.reshape(1, tokens),
        loss_mask.reshape(1, tokens),
        row_exp.reshape(lines, LANES),
        gain_exp,
        first_w,
        second_w,
        first_g.reshape(halves, 1, LANES),
        second_g.reshape(halves, 1, LANES),
        )]
    )
    new_weight, new_gain, first_w_new, second_w_new, first_g_new, second_g_new = pl.pallas_call(
        send_home,
        out_shape=shapes,
        in_specs=[vmem] * 6,
        out_specs=(hbm,) * 6,
        scratch_shapes=[dma((6,))],
        compiler_params=pltpu.CompilerParams(vmem_limit_bytes=8 << 20),
    )(*updated)
    return (
        new_weight.reshape(n_pipe * rows, bins),
        new_gain.reshape(-1),
        first_w_new,
        second_w_new,
        first_g_new.reshape(-1),
        second_g_new.reshape(-1),
    )


def any_shards(*args):
    hidden, head, first_g = args[0], args[1], args[10]
    fits = lax.axis_size("dp") == 2 and lax.axis_size("node") == 4 and lax.axis_size("pipe") > 1
    fits = fits and first_g.shape[0] % LANES == 0 and head.shape[1] == LANES
    fits = fits and hidden.shape[0] % LANES == 0 and hidden.shape[1] % 1024 == 0
    return fused_shards(*args) if fits else shards(*args)


def solution(mesh):
    return jax.shard_map(
        any_shards,
        mesh=mesh,
        in_specs=(
            P(("dp", "node", "pipe"), None),
            P(),
            P(),
            P(("dp", "node", "pipe")),
            P(("dp", "node", "pipe")),
            P(("dp", "node", "pipe")),
            P(("dp", "node", "pipe"), None),
            P(("dp", "node", "pipe"), None),
            P(("dp", "node", "pipe"), None),
            P(("dp", "node", "pipe"), None),
            P(("dp", "node", "pipe")),
            P(("dp", "node", "pipe")),
        ),
        out_specs=(
            P(("dp", "node"), None),
            P(("dp", "node")),
            P(("dp", "node", "pipe"), None),
            P(("dp", "node", "pipe"), None),
            P(("dp", "node", "pipe")),
            P(("dp", "node", "pipe")),
        ),
        check_vma=False,
    )
```

```python
import functools
import math

import jax
import jax.numpy as jnp
from jax import lax
from jax.experimental import pallas as pl
from jax.experimental.pallas import tpu as pltpu
from jax.sharding import PartitionSpec as P

BINS = 128
GBLK = 128
SEQ = 32


LOGIT_SCALE = 0.0625
RETURN_LOW = -4.0
RETURN_HIGH = 4.0
TRACE_DECAY = 0.95
SAT_LIMIT = 448.0
LEARN_RATE = 0.02
FIRST_CORR = 0.19
SECOND_CORR = 0.0975
EPSILON = 1e-08
NORM_EPSILON = 1e-06


def gauss_targets(returns):
    width = (RETURN_HIGH - RETURN_LOW) / BINS
    spread = 0.75 * width
    bin_edges = RETURN_LOW + width * jnp.arange(BINS + 1).astype(jnp.float32)
    clamped = jnp.clip(returns, RETURN_LOW, RETURN_HIGH)
    cum_mass = 0.5 * (
        1.0
        + jax.scipy.special.erf((bin_edges[None, :] - clamped[:, None]) / (spread * math.sqrt(2.0)))
    )
    bin_mass = cum_mass[:, 1:] - cum_mass[:, :-1]
    return bin_mass / (cum_mass[:, -1:] - cum_mass[:, :1])


def gae_returns(rewards, old_values):
    reward_rows = rewards.reshape(-1, SEQ)
    value_rows = old_values.reshape(-1, SEQ)
    following = jnp.concatenate(
        [value_rows[:, 1:], jnp.zeros((value_rows.shape[0], 1), jnp.float32)], axis=1
    )
    td_error = reward_rows + following - value_rows
    row_pos = lax.broadcasted_iota(jnp.int32, (SEQ, SEQ), 0)
    col_pos = lax.broadcasted_iota(jnp.int32, (SEQ, SEQ), 1)
    offset = jnp.maximum(row_pos - col_pos, 0).astype(jnp.float32)
    kernel = jnp.where(row_pos >= col_pos, jnp.power(TRACE_DECAY, offset), 0.0)
    traced = jnp.dot(td_error, kernel, precision=lax.Precision.HIGHEST)
    return (traced + value_rows).reshape(-1)


def local_terms(hidden, gain, head, targets, mask, row_scale_exp, block_scale_exp):
    hidden_f = hidden.astype(jnp.float32)
    inv_rms = lax.rsqrt(jnp.mean(hidden_f * hidden_f, axis=1, keepdims=True) + NORM_EPSILON)
    normed = hidden_f * inv_rms
    scaled = (normed * gain.astype(jnp.float32)).astype(jnp.bfloat16)
    logits = LOGIT_SCALE * jnp.dot(scaled, head, preferred_element_type=jnp.float32)
    shifted = jnp.exp(logits - jnp.max(logits, axis=1, keepdims=True))
    probs_out = shifted / jnp.sum(shifted, axis=1, keepdims=True)
    errors = (LOGIT_SCALE * mask.astype(jnp.float32)[:, None] * (probs_out - targets)).astype(
        jnp.bfloat16
    )
    row_limit = SAT_LIMIT * jnp.exp2(row_scale_exp.astype(jnp.float32))
    block_limit = SAT_LIMIT * jnp.repeat(jnp.exp2(block_scale_exp.astype(jnp.float32)), GBLK)
    return inv_rms, errors, row_limit[None, :], block_limit[None, :]


def adam_update(param, grad, first, second):
    first_new = 0.9 * first + 0.1 * grad
    second_new = 0.95 * second + 0.05 * grad * grad
    update = first_new / FIRST_CORR / (jnp.sqrt(second_new / SECOND_CORR) + EPSILON)
    return (
        (param.astype(jnp.float32) - LEARN_RATE * update).astype(jnp.bfloat16),
        first_new,
        second_new,
    )


LANES = 128
GAIN_ROWS = 16
VMEM_GRANT = 40000000
NEAR_LAG = 4
FAR_LAG = 4
DONE_LAG = 4
MESH = pl.DeviceIdType.MESH


def far_first(size):
    ring = [min(step, size - step) for step in range(size)]
    return sorted(range(size), key=lambda step: -ring[step])


def exchange(
    sizes,
    rows,
    hidden,
    inv_rms,
    errors_in,
    head,
    gain,
    row_limit,
    gain_limit,
    gain_blocks,
    first_w,
    second_w,
    first_g,
    second_g,
    new_weight,
    new_gain,
    first_w_new,
    second_w_new,
    first_g_new,
    second_g_new,
    quant,
    dp_buf,
    part,
    node_buf,
    pipe_out,
    pipe_buf,
    shared,
    dp_send,
    dp_recv,
    node_send,
    node_recv,
    pipe_send,
    pipe_recv,
    all_send,
    all_recv,
):
    n_dp, n_node, n_pipe = sizes
    me_dp = lax.axis_index("dp")
    me_node = lax.axis_index("node")
    me_pipe = lax.axis_index("pipe")
    gain_rows = first_g.shape[0]

    barrier = pltpu.get_barrier_semaphore()
    for axis, size, me in (("dp", n_dp, me_dp), ("node", n_node, me_node), ("pipe", n_pipe, me_pipe)):
        for step in range(1, size):
            pl.semaphore_signal(
                barrier, inc=1, device_id={axis: lax.rem(me + step, size)}, device_id_type=MESH
            )
    pl.semaphore_wait(barrier, n_dp + n_node + n_pipe - 3)

    order = far_first(n_pipe)

    def dp_copy(chunk, step):
        peer = lax.rem(me_dp + step, n_dp)
        return pltpu.make_async_remote_copy(
            src_ref=quant.at[peer, lax.rem(me_pipe + order[chunk], n_pipe)],
            dst_ref=dp_buf.at[step - 1, chunk],
            send_sem=dp_send.at[step - 1, chunk],
            recv_sem=dp_recv.at[step - 1, chunk],
            device_id={"dp": peer},
            device_id_type=MESH,
        )

    def node_copy(chunk, step):
        peer = lax.rem(me_node + step, n_node)
        return pltpu.make_async_remote_copy(
            src_ref=part.at[chunk, peer],
            dst_ref=node_buf.at[step - 1, chunk],
            send_sem=node_send.at[step - 1, chunk],
            recv_sem=node_recv.at[step - 1, chunk],
            device_id={"node": peer},
            device_id_type=MESH,
        )

    def pipe_copy(chunk):
        return pltpu.make_async_remote_copy(
            src_ref=pipe_out.at[chunk],
            dst_ref=pipe_buf.at[chunk],
            send_sem=pipe_send.at[chunk],
            recv_sem=pipe_recv.at[chunk],
            device_id={"pipe": lax.rem(me_pipe + order[chunk], n_pipe)},
            device_id_type=MESH,
        )

    def all_copy(step):
        return pltpu.make_async_remote_copy(
            src_ref=shared.at[me_pipe],
            dst_ref=shared.at[me_pipe],
            send_sem=all_send.at[step - 1],
            recv_sem=all_recv.at[step - 1],
            device_id={"pipe": lax.rem(me_pipe + step, n_pipe)},
            device_id_type=MESH,
        )

    tokens = hidden.shape[0]
    pad_rows = quant.shape[3] - rows
    errors = errors_in[...]
    errors_t = errors.astype(jnp.float32).T.astype(jnp.bfloat16)
    inverse = jnp.broadcast_to(inv_rms[...], (tokens, LANES))
    pad_index = lax.broadcasted_iota(jnp.int32, (pad_rows, LANES), 0)

    def multiply(dp, node, first_pipe, count):
        width = count * rows
        start = pl.multiple_of(((dp * n_node + node) * n_pipe + first_pipe) * rows, width)
        columns = pl.ds(start, width)
        normed = hidden[:, columns].astype(jnp.float32) * jnp.tile(inverse, (1, width // LANES))
        scaled = (normed * gain[:, columns]).astype(jnp.bfloat16)
        weight_t = jnp.dot(errors_t, scaled, preferred_element_type=jnp.float32)
        limit = row_limit[:, columns]
        weight = jnp.clip(weight_t, -limit, limit).T.astype(jnp.bfloat16)
        back_prop = lax.dot_general(
            errors, head[columns, :], (((1,), (1,)), ((), ())), preferred_element_type=jnp.float32
        )
        gain_part = jnp.sum(back_prop * normed, axis=0, keepdims=True)
        limit = gain_limit[:, columns]
        gain_part = jnp.clip(gain_part, -limit, limit)
        for index in range(count):
            pipe = first_pipe + index
            quant[dp, pipe, node, 0:rows] = weight[index * rows : (index + 1) * rows]
            padded = jnp.zeros((pad_rows, LANES), jnp.float32)
            for row in range(gain_rows):
                low = index * rows + row * LANES
                taken = min(LANES, rows - row * LANES)
                line = gain_part[:, low : low + taken]
                if taken < LANES:
                    line = jnp.concatenate([line, jnp.zeros((1, LANES - taken), jnp.float32)], axis=1)
                padded = jnp.where(pad_index == row, line, padded)
            quant[dp, pipe, node, rows : rows + pad_rows] = padded.astype(jnp.bfloat16)

    aligned = rows % LANES == 0

    def multiply_chunk(step, chunk):
        dp = lax.rem(me_dp + step, n_dp)
        if aligned:
            pipe = lax.rem(me_pipe + order[chunk], n_pipe)
            lax.fori_loop(0, n_node, lambda node, _: (multiply(dp, node, pipe, 1), _)[1], 0)
        elif chunk == 0:
            lax.fori_loop(0, n_node, lambda node, _: (multiply(dp, node, 0, n_pipe), _)[1], 0)

    for chunk in range(n_pipe):
        for step in range(1, n_dp):
            multiply_chunk(step, chunk)
            dp_copy(chunk, step).start()

    def dp_sum(chunk):
        own = lax.rem(me_pipe + order[chunk], n_pipe)
        multiply_chunk(0, chunk)
        for step in range(1, n_dp):
            dp_copy(chunk, step).wait_recv()
        for away in range(1, n_node + 1):
            node = lax.rem(me_node + away, n_node)
            total = quant[me_dp, own, node].astype(jnp.float32)
            for step in range(1, n_dp):
                total = total + dp_buf[step - 1, chunk, node].astype(jnp.float32)
            part[chunk, node] = total.astype(jnp.bfloat16)
            if away < n_node:
                node_copy(chunk, away).start()

    def node_sum(chunk):
        for step in range(1, n_node):
            node_copy(chunk, step).wait_recv()
        total = part[chunk, me_node].astype(jnp.float32)
        for step in range(1, n_node):
            total = total + node_buf[step - 1, chunk].astype(jnp.float32)
        pipe_out[chunk] = total.astype(jnp.bfloat16)
        if order[chunk] != 0:
            pipe_copy(chunk).start()

    for chunk in range(n_pipe):
        dp_sum(chunk)
        if chunk >= 1:
            node_sum(chunk - 1)
    node_sum(n_pipe - 1)

    for chunk in range(n_pipe - 1):
        pipe_copy(chunk).wait_recv()

    def adam(start, count, param, first, second, first_out, second_out):
        grad = pipe_out[n_pipe - 1, start : start + count].astype(jnp.float32)
        for chunk in range(n_pipe - 1):
            grad = grad + pipe_buf[chunk, start : start + count].astype(jnp.float32)
        new, first_new, second_new = adam_update(param, grad, first[...], second[...])
        first_out[...] = first_new
        second_out[...] = second_new
        return new

    position = (me_dp * n_node + me_node) * n_pipe + me_pipe
    own_weight = head[pl.ds(pl.multiple_of(position * rows, rows), rows), :]
    shared[me_pipe, rows : rows + gain_rows] = adam(
        rows, gain_rows, gain_blocks[position], first_g, second_g, first_g_new, second_g_new
    )
    shared[me_pipe, 0:rows] = adam(
        0, rows, own_weight, first_w, second_w, first_w_new, second_w_new
    )
    for step in range(1, n_pipe):
        all_copy(step).start()
    for chunk in range(n_pipe):
        for step in range(1, n_dp):
            dp_copy(chunk, step).wait_send()
        for step in range(1, n_node):
            node_copy(chunk, step).wait_send()
        if order[chunk] != 0:
            pipe_copy(chunk).wait_send()
    for step in range(1, n_pipe):
        all_copy(step).wait()
    for pipe in range(n_pipe):
        new_weight[pipe] = shared[pipe, 0:rows]
        new_gain[pipe] = shared[pipe, rows : rows + gain_rows]


def write_out(*refs):
    half = len(refs) // 2
    for source, target in zip(refs[:half], refs[half:]):
        target[...] = source[...]


def shards(
    final_hidden,
    value_head,
    norm_gain,
    rewards,
    old_values,
    loss_mask,
    row_exp,
    gain_exp,
    first_w,
    second_w,
    first_g,
    second_g,
):
    targets = gauss_targets(gae_returns(rewards, old_values))
    inv_rms, errors, row_limit, gain_limit = local_terms(
        final_hidden, norm_gain, value_head, targets, loss_mask, row_exp[0], gain_exp[0]
    )
    sizes = tuple(lax.axis_size(axis) for axis in ("dp", "node", "pipe"))
    n_dp, n_node, n_pipe = sizes
    rows = first_g.shape[0]
    bins = value_head.shape[1]
    gain_rows = -(-rows // bins)
    block_rows = rows + -(-gain_rows // GAIN_ROWS) * GAIN_ROWS

    def to_rows(values, total):
        lead = values.shape[:-1]
        values = jnp.pad(values, [(0, 0)] * len(lead) + [(0, total * bins - rows)])
        return values.reshape(lead + (total, bins))

    block = (block_rows, bins)
    vmem = pl.BlockSpec(memory_space=pltpu.VMEM)
    f32 = jnp.float32
    bf16 = jnp.bfloat16
    shapes = (
        jax.ShapeDtypeStruct((n_pipe, rows, bins), bf16),
        jax.ShapeDtypeStruct((n_pipe, gain_rows, bins), bf16),
        jax.ShapeDtypeStruct((rows, bins), f32),
        jax.ShapeDtypeStruct((rows, bins), f32),
        jax.ShapeDtypeStruct((gain_rows, bins), f32),
        jax.ShapeDtypeStruct((gain_rows, bins), f32),
    )
    buffers = [
        (n_dp, n_pipe, n_node) + block,
        (n_dp - 1, n_pipe, n_node) + block,
        (n_pipe, n_node) + block,
        (n_node - 1, n_pipe) + block,
        (n_pipe,) + block,
        (n_pipe,) + block,
        (n_pipe,) + block,
    ]
    held = 2 * sum(math.prod(shape) for shape in buffers)
    held += 2 * (final_hidden.size + value_head.size) + 24 * rows * bins
    updated = pl.pallas_call(
        functools.partial(exchange, sizes, rows),
        out_shape=shapes,
        in_specs=[vmem] * 12,
        out_specs=(vmem,) * 6,
        scratch_shapes=[pltpu.VMEM(shape, bf16) for shape in buffers]
        + [
            pltpu.SemaphoreType.DMA((n_dp - 1, n_pipe)),
            pltpu.SemaphoreType.DMA((n_dp - 1, n_pipe)),
            pltpu.SemaphoreType.DMA((n_node - 1, n_pipe)),
            pltpu.SemaphoreType.DMA((n_node - 1, n_pipe)),
            pltpu.SemaphoreType.DMA((n_pipe,)),
            pltpu.SemaphoreType.DMA((n_pipe,)),
            pltpu.SemaphoreType.DMA((n_pipe - 1,)),
            pltpu.SemaphoreType.DMA((n_pipe - 1,)),
        ],
        compiler_params=pltpu.CompilerParams(
            collective_id=0, has_side_effects=True, vmem_limit_bytes=held + (12 << 20)
        ),
    )(
        final_hidden,
        inv_rms,
        errors,
        value_head,
        norm_gain.astype(f32)[None, :],
        row_limit,
        gain_limit,
        to_rows(norm_gain.reshape(-1, rows), gain_rows),
        first_w,
        second_w,
        to_rows(first_g, gain_rows),
        to_rows(second_g, gain_rows),
    )
    new_weight, new_gain, first_w_new, second_w_new, first_g_new, second_g_new = pl.pallas_call(
        write_out,
        out_shape=shapes,
        in_specs=[vmem] * 6,
        out_specs=(vmem,) * 6,
        compiler_params=pltpu.CompilerParams(vmem_limit_bytes=8 << 20),
    )(*updated)

    def from_rows(values):
        lead = values.shape[:-2]
        return values.reshape(lead + (gain_rows * bins,))[..., :rows].reshape(-1)

    return (
        new_weight.reshape(n_pipe * rows, bins),
        from_rows(new_gain),
        first_w_new,
        second_w_new,
        from_rows(first_g_new),
        from_rows(second_g_new),
    )


def ahead(n_pipe, me_pipe, step):
    return lax.rem(me_pipe + step, n_pipe)


def fused(
    sizes,
    rows,
    hidden_in,
    head_in,
    gain_in,
    rewards_in,
    values_in,
    mask_in,
    row_exp_in,
    gain_exp_in,
    first_w_in,
    second_w_in,
    first_g_in,
    second_g_in,
    new_weight,
    new_gain,
    first_w_new,
    second_w_new,
    first_g_new,
    second_g_new,
    hidden,
    head,
    gain_raw,
    rewards,
    values,
    mask,
    row_exp,
    gain_exp,
    first_w,
    second_w,
    first_g,
    second_g,
    gain,
    row_limit,
    gain_limit,
    quant,
    dp_buf,
    part,
    near_buf,
    far_out,
    far_buf,
    held,
    pipe_out,
    pipe_buf,
    own,
    gain_quant,
    gain_dp,
    gain_part,
    gain_node,
    gain_sum,
    gain_pipe,
    gain_all,
    load_sem,
    hidden_sem,
    head_sem,
    dp_send,
    dp_recv,
    near_send,
    near_recv,
    far_send,
    far_recv,
    pipe_send,
    pipe_recv,
    all_send,
    all_recv,
    gain_send,
    gain_recv,
):
    n_dp, n_node, n_pipe = sizes
    me_dp = lax.axis_index("dp")
    me_node = lax.axis_index("node")
    me_pipe = lax.axis_index("pipe")
    me_high, me_low = me_node // 2, lax.rem(me_node, 2)
    f32, bf16 = jnp.float32, jnp.bfloat16
    halves = rows // LANES
    tokens, width = hidden.shape
    bins = head.shape[1]
    chunks = hidden_sem.shape[0]
    step_width = width // chunks
    peer_dp = 1 - me_dp

    small = (
        (rewards_in, rewards),
        (values_in, values),
        (mask_in, mask),
        (gain_in, gain_raw),
        (row_exp_in, row_exp),
        (gain_exp_in, gain_exp),
        (first_w_in, first_w),
        (second_w_in, second_w),
        (first_g_in, first_g),
        (second_g_in, second_g),
    )
    loads = [pltpu.make_async_copy(*pair, load_sem.at[index]) for index, pair in enumerate(small)]
    hidden_loads = []
    head_loads = []
    for chunk in range(chunks):
        span = pl.ds(chunk * step_width, step_width)
        hidden_loads.append(
            pltpu.make_async_copy(hidden_in.at[:, span], hidden.at[:, span], hidden_sem.at[chunk])
        )
        head_loads.append(
            pltpu.make_async_copy(head_in.at[span, :], head.at[span, :], head_sem.at[chunk])
        )
    for copy in loads[:4]:
        copy.start()
    for chunk in range(chunks):
        hidden_loads[chunk].start()
        head_loads[chunk].start()
    for copy in loads[4:]:
        copy.start()

    barrier = pltpu.get_barrier_semaphore()
    for axis, size, me in (("dp", n_dp, me_dp), ("node", n_node, me_node), ("pipe", n_pipe, me_pipe)):
        for step in range(1, size):
            pl.semaphore_signal(
                barrier, inc=1, device_id={axis: lax.rem(me + step, size)}, device_id_type=MESH
            )

    for copy in loads[:4]:
        copy.wait()
    at = lax.broadcasted_iota(jnp.int32, (tokens, tokens), 0)
    later = lax.broadcasted_iota(jnp.int32, (tokens, tokens), 1)
    reach = jnp.where(at // SEQ == later // SEQ, later - at, -1)
    decay = jnp.exp(jnp.maximum(reach, 0).astype(f32) * math.log(TRACE_DECAY))
    reward_part = jnp.where(reach >= 0, decay, 0.0) * rewards[...]
    value_part = jnp.where(reach > 0, decay * ((1.0 - TRACE_DECAY) / TRACE_DECAY), 0.0) * values[...]
    returns = jnp.sum(reward_part + value_part, axis=1, keepdims=True)
    returns = jnp.clip(returns, RETURN_LOW, RETURN_HIGH)
    counted = jnp.sum(
        jnp.where(at == later, mask[...].astype(f32), 0.0), axis=1, keepdims=True
    )
    bin_width = (RETURN_HIGH - RETURN_LOW) / bins
    sharp = 1.0 / (0.75 * bin_width * math.sqrt(2.0))
    edge = lax.broadcasted_iota(jnp.int32, (tokens, bins), 1).astype(f32) * bin_width + RETURN_LOW
    low_mass = lax.erf((edge - returns) * sharp)
    high_mass = lax.erf((edge + bin_width - returns) * sharp)
    targets = (high_mass - low_mass) / (high_mass[:, bins - 1 :] - low_mass[:, :1])
    gain[...] = gain_raw[...].astype(f32)

    groups = step_width // LANES
    squares = jnp.zeros((tokens, LANES), f32)
    logits = jnp.zeros((tokens, bins), f32)
    for chunk in range(chunks):
        hidden_loads[chunk].wait()
        head_loads[chunk].wait()
        pieces = []
        for group in range(groups):
            low = chunk * step_width + group * LANES
            piece = hidden[:, low : low + LANES].astype(f32)
            squares = squares + piece * piece
            line = low // LANES
            pieces.append((piece * gain[line : line + 1, :]).astype(bf16))
        logits = logits + jnp.dot(
            jnp.concatenate(pieces, axis=1),
            head[chunk * step_width : (chunk + 1) * step_width, :],
            preferred_element_type=f32,
        )
    for copy in loads[4:]:
        copy.wait()
    row_limit[...] = SAT_LIMIT * jnp.exp2(row_exp[...].astype(f32))
    lines = gain.shape[0]
    line_at = lax.broadcasted_iota(jnp.int32, (lines, lines), 0)
    line_of = lax.broadcasted_iota(jnp.int32, (lines, lines), 1)
    block_limit = SAT_LIMIT * jnp.exp2(gain_exp[...].astype(f32))
    block_limit = jnp.sum(jnp.where(line_at == line_of, block_limit, 0.0), axis=1, keepdims=True)
    gain_limit[...] = jnp.broadcast_to(block_limit, (lines, LANES))

    mean_square = jnp.sum(squares, axis=1, keepdims=True) * (1.0 / width)
    inv_rms = lax.rsqrt(mean_square + NORM_EPSILON)
    logits = logits * (inv_rms * LOGIT_SCALE)
    shifted = jnp.exp(logits - jnp.max(logits, axis=1, keepdims=True))
    probs = shifted / jnp.sum(shifted, axis=1, keepdims=True)
    scaled_errors = (counted * inv_rms * LOGIT_SCALE) * (probs - targets)
    errors = scaled_errors.astype(bf16)
    errors_t = scaled_errors.T.astype(bf16)

    pl.semaphore_wait(barrier, n_dp + n_node + n_pipe - 3)

    order = far_first(n_pipe)
    phases = [(half, slot) for half in range(halves) for slot in range(n_pipe)]

    def remote(source, target, send, recv, device_id):
        return pltpu.make_async_remote_copy(
            src_ref=source,
            dst_ref=target,
            send_sem=send,
            recv_sem=recv,
            device_id=device_id,
            device_id_type=MESH,
        )

    def dp_copy(half, slot):
        return remote(
            quant.at[peer_dp, half, slot],
            dp_buf.at[half, slot],
            dp_send.at[half, slot],
            dp_recv.at[half, slot],
            {"dp": peer_dp},
        )

    def low_first(slot):
        return slot % 2 == 0

    def low_peer():
        return me_high * 2 + 1 - me_low

    def high_peer():
        return (1 - me_high) * 2 + me_low

    def near_copy(half, slot):
        if low_first(slot):
            source, peer = part.at[half, slot, :, 1 - me_low], low_peer()
        else:
            source, peer = part.at[half, slot, 1 - me_high], high_peer()
        return remote(
            source,
            near_buf.at[half, slot],
            near_send.at[half, slot],
            near_recv.at[half, slot],
            {"node": peer},
        )

    def far_copy(half, slot):
        return remote(
            far_out.at[half, slot],
            far_buf.at[half, slot],
            far_send.at[half, slot],
            far_recv.at[half, slot],
            {"node": high_peer() if low_first(slot) else low_peer()},
        )

    def pipe_copy(half, slot):
        return remote(
            pipe_out.at[half, slot],
            pipe_buf.at[half, slot],
            pipe_send.at[half, slot],
            pipe_recv.at[half, slot],
            {"pipe": ahead(n_pipe, me_pipe, order[slot])},
        )

    def all_copy(half, slot):
        return remote(
            new_weight.at[me_pipe, half],
            new_weight.at[me_pipe, half],
            all_send.at[half, slot],
            all_recv.at[half, slot],
            {"pipe": ahead(n_pipe, me_pipe, order[slot])},
        )

    def gain_copy(source, target, index, device_id):
        return remote(source, target, gain_send.at[index], gain_recv.at[index], device_id)

    gain_dp_copy = gain_copy(gain_quant.at[peer_dp], gain_dp, 0, {"dp": peer_dp})
    gain_node_copies = []
    for step in range(1, n_node):
        peer = lax.rem(me_node + step, n_node)
        gain_node_copies.append(
            gain_copy(gain_part.at[peer], gain_node.at[step - 1], step, {"node": peer})
        )
    gain_pipe_copies = []
    gain_all_copies = []
    for step in range(1, n_pipe):
        peer = ahead(n_pipe, me_pipe, step)
        gain_pipe_copies.append(
            gain_copy(
                gain_sum.at[peer], gain_pipe.at[step - 1], n_node + step - 1, {"pipe": peer}
            )
        )
        gain_all_copies.append(
            gain_copy(
                gain_all.at[me_pipe],
                gain_all.at[me_pipe],
                n_node + n_pipe + step - 2,
                {"pipe": peer},
            )
        )

    def multiply(dp, slot):
        pipe = ahead(n_pipe, me_pipe, order[slot])
        for node in range(n_node):
            block = (dp * n_node + node) * n_pipe + pipe
            span = pl.ds(pl.multiple_of(block * rows, rows), rows)
            columns = hidden[:, span]
            weight_t = jnp.dot(errors_t, columns, preferred_element_type=f32)
            back_prop = lax.dot_general(
                errors, head[span, :], (((1,), (1,)), ((), ())), preferred_element_type=f32
            )
            gain_line = jnp.sum(back_prop * columns.astype(f32), axis=0, keepdims=True)
            for half in range(halves):
                line = pl.ds(block * halves + half, 1)
                low = half * LANES
                limit = row_limit[line, :]
                weight = weight_t[:, low : low + LANES] * gain[line, :]
                quant[dp, half, slot, node // 2, node % 2] = jnp.clip(
                    weight, -limit, limit
                ).astype(bf16)
                limit = gain_limit[line, :]
                taken = jnp.clip(gain_line[:, low : low + LANES], -limit, limit)
                gain_quant[dp, node, pipe, half] = taken.astype(bf16).astype(f32)

    def add_dp(half, slot):
        dp_copy(half, slot).wait_recv()
        total = quant[me_dp, half, slot].astype(f32) + dp_buf[half, slot].astype(f32)
        part[half, slot] = total.astype(bf16)
        near_copy(half, slot).start()

    def add_near(half, slot):
        near_copy(half, slot).wait_recv()
        if low_first(slot):
            sent, kept = part[half, slot, 1 - me_high, me_low], part[half, slot, me_high, me_low]
            other, mine = 1 - me_high, me_high
        else:
            sent, kept = part[half, slot, me_high, 1 - me_low], part[half, slot, me_high, me_low]
            other, mine = 1 - me_low, me_low
        total = sent.astype(f32) + near_buf[half, slot, other].astype(f32)
        far_out[half, slot] = total.astype(bf16)
        far_copy(half, slot).start()
        held[half, slot] = kept.astype(f32) + near_buf[half, slot, mine].astype(f32)

    def add_far(half, slot):
        far_copy(half, slot).wait_recv()
        total = held[half, slot] + far_buf[half, slot].astype(f32)
        if order[slot] == 0:
            own[half] = total
        else:
            pipe_out[half, slot] = total.astype(bf16)
            pipe_copy(half, slot).start()

    position = (me_dp * n_node + me_node) * n_pipe + me_pipe

    def finish(half):
        total = own[half]
        for slot in range(n_pipe):
            if order[slot] != 0:
                pipe_copy(half, slot).wait_recv()
                total = total + pipe_buf[half, slot].astype(f32)
        low = half * LANES
        start = pl.multiple_of(position * rows + low, LANES)
        new, first, second = adam_update(
            head[pl.ds(start, LANES), :],
            total.T,
            first_w[low : low + LANES, :],
            second_w[low : low + LANES, :],
        )
        new_weight[me_pipe, half] = new
        for slot in range(n_pipe):
            if order[slot] != 0:
                all_copy(half, slot).start()
        first_w_new[low : low + LANES, :] = first
        second_w_new[low : low + LANES, :] = second

    def gain_add_dp():
        gain_dp_copy.wait_recv()
        gain_part[...] = gain_quant[me_dp] + gain_dp[...]
        for copy in gain_node_copies:
            copy.start()

    def gain_add_node():
        total = gain_part[me_node]
        for index, copy in enumerate(gain_node_copies):
            copy.wait_recv()
            total = total + gain_node[index]
        gain_sum[...] = total
        for copy in gain_pipe_copies:
            copy.start()

    def gain_finish():
        total = gain_sum[me_pipe]
        for index, copy in enumerate(gain_pipe_copies):
            copy.wait_recv()
            total = total + gain_pipe[index]
        for half in range(halves):
            param = gain[pl.ds(position * halves + half, 1), :]
            new, first, second = adam_update(param, total[half], first_g[half], second_g[half])
            gain_all[me_pipe, half] = new.astype(f32)
            first_g_new[half] = first
            second_g_new[half] = second
        for copy in gain_all_copies:
            copy.start()

    for slot in range(n_pipe):
        multiply(peer_dp, slot)
        for half in range(halves):
            dp_copy(half, slot).start()
    gain_dp_copy.start()
    count = len(phases)
    near_lag = min(NEAR_LAG, count)
    far_lag = near_lag + min(FAR_LAG, count)

    def advance(index):
        if index < count:
            add_dp(*phases[index])
        if 0 <= index - near_lag < count:
            add_near(*phases[index - near_lag])
            if index - near_lag == n_pipe:
                gain_add_node()
        if 0 <= index - far_lag < count:
            add_far(*phases[index - far_lag])
            if index - far_lag == n_pipe:
                gain_finish()
        for half in range(halves - 1):
            if index - far_lag == min(half * n_pipe + n_pipe - 1 + DONE_LAG, count - 1):
                finish(half)

    for slot in range(n_pipe):
        multiply(me_dp, slot)
        advance(slot)
    gain_add_dp()
    for index in range(n_pipe, count + far_lag):
        advance(index)
    finish(halves - 1)

    for half, slot in phases:
        dp_copy(half, slot).wait_send()
        near_copy(half, slot).wait_send()
        far_copy(half, slot).wait_send()
        if order[slot] != 0:
            pipe_copy(half, slot).wait_send()
    gain_dp_copy.wait_send()
    for copy in gain_node_copies + gain_pipe_copies:
        copy.wait_send()
    for copy in gain_all_copies:
        copy.wait()
    new_gain[...] = gain_all[...].reshape(n_pipe * halves, LANES).astype(bf16)
    for half, slot in phases:
        if order[slot] != 0:
            all_copy(half, slot).wait()


def send_home(*refs):
    count = (len(refs) - 1) // 2
    sems = refs[-1]
    copies = [
        pltpu.make_async_copy(refs[index], refs[count + index], sems.at[index])
        for index in range(count)
    ]
    for copy in copies:
        copy.start()
    for copy in copies:
        copy.wait()


def fused_shards(
    final_hidden,
    value_head,
    norm_gain,
    rewards,
    old_values,
    loss_mask,
    row_exp,
    gain_exp,
    first_w,
    second_w,
    first_g,
    second_g,
):
    sizes = tuple(lax.axis_size(axis) for axis in ("dp", "node", "pipe"))
    n_dp, n_node, n_pipe = sizes
    rows = first_g.shape[0]
    tokens, width = final_hidden.shape
    bins = value_head.shape[1]
    halves = rows // LANES
    lines = width // LANES
    chunks = max(1, width // 1024)
    f32, bf16, i32 = jnp.float32, jnp.bfloat16, jnp.int32
    vmem = pl.BlockSpec(memory_space=pltpu.VMEM)
    hbm = pl.BlockSpec(memory_space=pltpu.HBM)
    tile = (bins, LANES)
    shapes = (
        jax.ShapeDtypeStruct((n_pipe, halves, LANES, bins), bf16),
        jax.ShapeDtypeStruct((n_pipe * halves, LANES), bf16),
        jax.ShapeDtypeStruct((rows, bins), f32),
        jax.ShapeDtypeStruct((rows, bins), f32),
        jax.ShapeDtypeStruct((halves, 1, LANES), f32),
        jax.ShapeDtypeStruct((halves, 1, LANES), f32),
    )
    buffers = [
        ((tokens, width), bf16),
        ((width, bins), bf16),
        ((lines, LANES), bf16),
        ((1, tokens), f32),
        ((1, tokens), f32),
        ((1, tokens), i32),
        ((lines, LANES), i32),
        ((1, lines), i32),
        ((rows, bins), f32),
        ((rows, bins), f32),
        ((halves, 1, LANES), f32),
        ((halves, 1, LANES), f32),
        ((lines, LANES), f32),
        ((lines, LANES), f32),
        ((lines, LANES), f32),
        ((n_dp, halves, n_pipe, 2, 2) + tile, bf16),
        ((halves, n_pipe, 2, 2) + tile, bf16),
        ((halves, n_pipe, 2, 2) + tile, bf16),
        ((halves, n_pipe, 2) + tile, bf16),
        ((halves, n_pipe) + tile, bf16),
        ((halves, n_pipe) + tile, bf16),
        ((halves, n_pipe) + tile, f32),
        ((halves, n_pipe) + tile, bf16),
        ((halves, n_pipe) + tile, bf16),
        ((halves,) + tile, f32),
        ((n_dp, n_node, n_pipe, halves, 1, LANES), f32),
        ((n_node, n_pipe, halves, 1, LANES), f32),
        ((n_node, n_pipe, halves, 1, LANES), f32),
        ((n_node - 1, n_pipe, halves, 1, LANES), f32),
        ((n_pipe, halves, 1, LANES), f32),
        ((n_pipe - 1, halves, 1, LANES), f32),
        ((n_pipe, halves, 1, LANES), f32),
    ]
    dma = pltpu.SemaphoreType.DMA
    semaphores = [(10,), (chunks,), (chunks,)]
    semaphores += [(halves, n_pipe)] * 10
    semaphores += [(n_node + 2 * n_pipe - 2,)] * 2
    updated = pl.pallas_call(
        functools.partial(fused, sizes, rows),
        out_shape=shapes,
        in_specs=[hbm] * 12,
        out_specs=(vmem,) * 6,
        scratch_shapes=[pltpu.VMEM(shape, kind) for shape, kind in buffers]
        + [dma(shape) for shape in semaphores],
        compiler_params=pltpu.CompilerParams(
            collective_id=0, has_side_effects=True, vmem_limit_bytes=VMEM_GRANT
        ),
    )(
        *[pltpu.with_memory_space_constraint(value, pltpu.HBM) for value in (
        final_hidden,
        value_head,
        norm_gain.reshape(lines, LANES),
        rewards.reshape(1, tokens),
        old_values.reshape(1, tokens),
        loss_mask.reshape(1, tokens),
        row_exp.reshape(lines, LANES),
        gain_exp,
        first_w,
        second_w,
        first_g.reshape(halves, 1, LANES),
        second_g.reshape(halves, 1, LANES),
        )]
    )
    new_weight, new_gain, first_w_new, second_w_new, first_g_new, second_g_new = pl.pallas_call(
        send_home,
        out_shape=shapes,
        in_specs=[vmem] * 6,
        out_specs=(hbm,) * 6,
        scratch_shapes=[dma((6,))],
        compiler_params=pltpu.CompilerParams(vmem_limit_bytes=8 << 20),
    )(*updated)
    return (
        new_weight.reshape(n_pipe * rows, bins),
        new_gain.reshape(-1),
        first_w_new,
        second_w_new,
        first_g_new.reshape(-1),
        second_g_new.reshape(-1),
    )


def any_shards(*args):
    hidden, head, first_g = args[0], args[1], args[10]
    fits = lax.axis_size("dp") == 2 and lax.axis_size("node") == 4 and lax.axis_size("pipe") == 4
    fits = fits and first_g.shape[0] % LANES == 0 and head.shape[1] == LANES
    fits = fits and hidden.shape[0] % LANES == 0 and hidden.shape[1] % 1024 == 0
    return fused_shards(*args) if fits else shards(*args)


def solution(mesh):
    return jax.shard_map(
        any_shards,
        mesh=mesh,
        in_specs=(
            P(("dp", "node", "pipe"), None),
            P(),
            P(),
            P(("dp", "node", "pipe")),
            P(("dp", "node", "pipe")),
            P(("dp", "node", "pipe")),
            P(("dp", "node", "pipe"), None),
            P(("dp", "node", "pipe"), None),
            P(("dp", "node", "pipe"), None),
            P(("dp", "node", "pipe"), None),
            P(("dp", "node", "pipe")),
            P(("dp", "node", "pipe")),
        ),
        out_specs=(
            P(("dp", "node"), None),
            P(("dp", "node")),
            P(("dp", "node", "pipe"), None),
            P(("dp", "node", "pipe"), None),
            P(("dp", "node", "pipe")),
            P(("dp", "node", "pipe")),
        ),
        check_vma=False,
    )
```
